128 devices in a mesh: dp: 16 (over y, x_lo, core), fsdp: 8 (over z, x_hi).
Axes of the slice: x: 4 (x_hi: 2, x_lo: 2; x = x_hi * 2 + x_lo), y: 4, z: 4, core: 2. Of those that a mesh axis runs over, the one named last changes fastest.
Arguments:
- hidden: bfloat16 [49152, 5120], P(('dp', 'fsdp')), may hold values from -6 to 6
- norm_gain: bfloat16 [5120], replicated, may hold values from 0.25 to 1.75
- q_weight: bfloat16 [5120, 2560], P('dp', 'fsdp')
- kv_weight: bfloat16 [5120, 1024], P('dp', 'fsdp')
- q_bias: bfloat16 [2560], replicated, may hold values from -3 to 3
- kv_bias: bfloat16 [1024], replicated, may hold values from -3 to 3
- segments: int32 [49152], P(('dp', 'fsdp')), may hold values from -1 to 383, as said below
Outputs:
- attention_context: bfloat16 [49152, 2560], P(('dp', 'fsdp'))
The draws below stay inside these ranges and needn't reach their ends.
Inputs may be any that keep to these rules, and one draw needn't show every extreme that they name: `segments`: in each device's run of 384 rows the live rows are its first whole blocks of 128; their ids start at 0 and never fall, each rollout has 1 to 256 rows, and somewhere in the slice one rollout has exactly 256; the other rows are -1. The devices at dp indices i and i + 16 / 2 with the same fsdp index hold exactly 4 live blocks together, and some device holds 3. Some device has 384 rollouts of one row each.
All inputs are finite; a program needn't handle non-finite values.
Results may differ from the reference program's by a relative error of at most 0.0058.
Values may be sent and summed in bfloat16 or wider, within the bound.
No kernel may reach another device: no remote copies, remote signals or barrier semaphores. Data moves between devices by JAX's collectives and lax.ppermute only.
A program may use at most 128 MiB of HBM per device.

```python
import jax
import jax.numpy as jnp
from jax import lax

D = 5120
HEADS = 20
KV_HEADS = 4
HEAD_DIM = 128
BLOCK = 128
SLOTS = 3
MOST = 256
TOTAL_ROWS = 49152
QCOLS = 2560
KVCOLS = 1024
N_DP = 16
N_FSDP = 8


def key_columns(key):
    return jax.random.normal(jax.random.fold_in(key, 7), (D, 2 * KV_HEADS * HEAD_DIM), jnp.float32) * D ** (-0.5)


def draw_kv_weight(key, part):
    return key_columns(key).astype(jnp.bfloat16)


def draw_q_weight(key, part):
    base = jax.random.normal(jax.random.fold_in(key, 11), (D, HEADS * HEAD_DIM), jnp.float32) * D ** (-0.5)
    return base.astype(jnp.bfloat16)


def draw_segments(key, part):
    half_slots = (SLOTS + 1) // 2
    row_count = SLOTS * BLOCK
    device_count = N_DP * N_FSDP
    lower_loads = jax.random.randint(jax.random.fold_in(key, 3), (N_DP // 2, N_FSDP), 1, SLOTS + 1)
    lower_loads = lower_loads.at[0, 0].set(SLOTS)
    lower_loads = lower_loads.at[0, 1].set(SLOTS)
    block_loads = jnp.concatenate([lower_loads, 2 * half_slots - lower_loads], axis=0).reshape(-1)
    row_ids = jnp.arange(row_count, dtype=jnp.int32)[None, :]
    device_ids = jnp.arange(device_count, dtype=jnp.int32)[:, None]
    die_rolls = jax.random.randint(jax.random.fold_in(key, 5), (device_count, row_count), 0, 96)
    random_starts = (die_rolls == 0) & jnp.logical_not((device_ids == 1) & (row_ids < MOST))
    starts = random_starts | (row_ids % MOST == 0) | (device_ids == 0)
    segment_ids = jnp.cumsum(starts.astype(jnp.int32), axis=1) - 1
    live_rows = row_ids < block_loads[:, None] * BLOCK
    return jnp.where(live_rows, segment_ids, -1).astype(jnp.int32).reshape(-1)


def level_of(stream_key, shape, shards, low, top_value):
    factor_of = 1.0
    for position, parts in shards:
        draws = jax.random.uniform(jax.random.fold_in(jax.random.fold_in(stream_key, 6), position), (parts,), jnp.float32, low / len(shards), top_value / len(shards))
        factor_of = factor_of * jnp.repeat(jnp.exp(draws), shape[position] // parts).reshape((-1,) + (1,) * (len(shape) - 1 - position))
    return factor_of


def noise(stream_key, dims, deviation, bound, split=(), kind=jnp.bfloat16):
    drawn = jax.random.normal(stream_key, dims, jnp.float32) * deviation
    if len(split) > 0:
        drawn = level_of(stream_key, dims, split, -0.22, 0.18) * drawn
    return jnp.clip(drawn, min=-bound, max=bound).astype(kind)


def setup_inputs(seed: int = 0) -> dict:
    splits = jax.random.split(jax.random.key(seed), 8)
    return {
        "hidden": noise(splits[0], (TOTAL_ROWS, D), 1.0, 6.0, ((0, 128),)),
        "norm_gain": jnp.clip(1.0 + 0.15 * jax.random.normal(splits[1], (D,), jnp.float32), 0.25, 1.75).astype(jnp.bfloat16),
        "q_weight": draw_q_weight(jax.random.fold_in(splits[7], 71), 0),
        "kv_weight": draw_kv_weight(jax.random.fold_in(splits[7], 71), 0),
        "q_bias": noise(splits[4], (QCOLS,), 0.5, 3.0),
        "kv_bias": noise(splits[5], (KVCOLS,), 0.5, 3.0),
        "segments": draw_segments(jax.random.fold_in(splits[7], 71), 0),
    }


def positions_of(segments):
    row_ids = jnp.arange(segments.shape[0], dtype=jnp.int32)
    before = jnp.concatenate([jnp.full((1,), -3, jnp.int32), segments[:-1]])
    starts = jnp.where(segments != before, row_ids, 0).astype(jnp.int32)
    return row_ids - lax.cummax(starts, axis=0)

def rotate(source, positions):
    half_dim = HEAD_DIM // 2
    frequency = jnp.exp(jnp.arange(half_dim, dtype=jnp.float32) * (-2.0 / HEAD_DIM) * jnp.log(jnp.float32(1000000.0)))
    angles = positions.astype(jnp.float32)[:, None] * frequency[None, :]
    cosine = jnp.cos(angles)[:, None, :]
    sine_part = jnp.sin(angles)[:, None, :]
    lower_half = source[..., :half_dim]
    second = source[..., half_dim:]
    return jnp.concatenate([lower_half * cosine - second * sine_part, second * cosine + lower_half * sine_part], axis=-1)

def normalize(hidden, norm_gain):
    as_float = hidden.astype(jnp.float32)
    mean_square = lax.optimization_barrier(jnp.mean(as_float * as_float, axis=-1, keepdims=True))
    return (as_float * lax.rsqrt(mean_square + 1e-06) * norm_gain.astype(jnp.float32)).astype(jnp.bfloat16)

def windows(source, fill_value):
    block_count = source.shape[0] // BLOCK
    shaped = source.reshape((block_count, BLOCK) + source.shape[1:])
    padded = jnp.concatenate([jnp.full((2,) + shaped.shape[1:], fill_value, source.dtype), shaped], axis=0)
    return jnp.concatenate([padded[0:block_count], padded[1:block_count + 1], padded[2:block_count + 2]], axis=1)

def attend(queries, key_rows, values, segments):
    row_count = queries.shape[0]
    block_count = row_count // BLOCK
    group_size = HEADS // KV_HEADS
    row_ids = jnp.arange(row_count, dtype=jnp.int32)
    key_win = windows(key_rows, 0).astype(jnp.float32)
    value_win = windows(values, 0).astype(jnp.float32)
    seg_win = windows(segments, -2)
    row_win = windows(row_ids, -1)
    q_blocks = queries.reshape(block_count, BLOCK, KV_HEADS, group_size, HEAD_DIM).astype(jnp.float32)
    scores = jnp.einsum('bqkgd,bskd->bkgqs', q_blocks, key_win, precision=lax.Precision.HIGHEST) * HEAD_DIM ** (-0.5)
    q_seg = segments.reshape(block_count, BLOCK)
    q_row = row_ids.reshape(block_count, BLOCK)
    allowed = (seg_win[:, None, :] == q_seg[:, :, None]) & (row_win[:, None, :] <= q_row[:, :, None]) & (q_seg[:, :, None] >= 0)
    scores = jnp.where(allowed[:, None, None], scores, -1e+30)
    row_max = lax.optimization_barrier(jnp.max(scores, axis=-1, keepdims=True))
    exponents = jnp.exp(scores - row_max)
    probabilities = (exponents / lax.optimization_barrier(jnp.sum(exponents, axis=-1, keepdims=True))).astype(jnp.bfloat16)
    context = jnp.einsum('bkgqs,bskd->bqkgd', probabilities.astype(jnp.float32), value_win, precision=lax.Precision.HIGHEST)
    context = jnp.where((q_seg >= 0)[:, :, None, None, None], context, 0.0)
    return context.reshape(row_count, HEADS * HEAD_DIM).astype(jnp.bfloat16)

def one_device(hidden, segments, norm_gain, q_weight, kv_weight, q_bias, kv_bias):
    row_count = hidden.shape[0]
    positions = positions_of(segments)
    normed = normalize(hidden, norm_gain)
    q_lin = jnp.dot(normed, q_weight, preferred_element_type=jnp.float32) + q_bias.astype(jnp.float32)
    kv_lin = jnp.dot(normed, kv_weight, preferred_element_type=jnp.float32) + kv_bias.astype(jnp.float32)
    split_at = KV_HEADS * HEAD_DIM
    queries = rotate(q_lin.reshape(row_count, HEADS, HEAD_DIM), positions).astype(jnp.bfloat16)
    key_rows = rotate(kv_lin[:, :split_at].reshape(row_count, KV_HEADS, HEAD_DIM), positions).astype(jnp.bfloat16)
    values = kv_lin[:, split_at:].reshape(row_count, KV_HEADS, HEAD_DIM).astype(jnp.bfloat16)
    return attend(queries, key_rows, values, segments)

def reference(hidden, norm_gain, q_weight, kv_weight, q_bias, kv_bias, segments):
    run_rows = SLOTS * BLOCK
    device_count = hidden.shape[0] // run_rows
    hidden_runs = hidden.reshape(device_count, run_rows, hidden.shape[1])
    segment_runs = segments.reshape(device_count, run_rows)

    def single(items):
        return one_device(items[0], items[1], norm_gain, q_weight, kv_weight, q_bias, kv_bias)
    output = lax.map(single, (hidden_runs, segment_runs))
    return output.reshape(device_count * run_rows, HEADS * HEAD_DIM)
```

```python
import jax
import jax.numpy as jnp
from jax import lax
from jax.experimental import pallas as pl
from jax.experimental.pallas import tpu as pltpu
from jax.sharding import Mesh, PartitionSpec as P

HEADS = 20
KV_HEADS = 4
HEAD_DIM = 128
ROWS = 384
D = 5120
AXES = ("y", "xl", "c", "z", "xh")
F32 = jnp.float32
BF16 = jnp.bfloat16


def pair_low(v):
    return v ^ 1


def pair_high(v):
    return (v + 1) % 4 if v % 2 else (v - 1) % 4


def pair_of(order, core):
    return pair_low if (order + core) % 2 == 0 else pair_high


def exchange_pairs(axis, order):
    pairs = []
    for y in range(4):
        for xl in range(2):
            for c in range(2):
                for z in range(4):
                    for xh in range(2):
                        move = pair_of(order, c)
                        ty, tx, tz = y, 2 * xh + xl, z
                        if axis == "x":
                            tx = move(tx)
                        elif axis == "y":
                            ty = move(ty)
                        else:
                            tz = move(tz)
                        src = (((y * 2 + xl) * 2 + c) * 4 + z) * 2 + xh
                        dst = (((ty * 2 + tx % 2) * 2 + c) * 4 + tz) * 2 + tx // 2
                        pairs.append((src, dst))
    return pairs


def traced_pair(v, order, core):
    low = v ^ 1
    high = jnp.where(v % 2 == 1, v + 1, v + 3) % 4
    return jnp.where((core + order) % 2 == 0, low, high)


def ring_source(v, core, first, second):
    if second:
        v = traced_pair(v, 1, core)
    if first:
        v = traced_pair(v, 0, core)
    return v


AXIS_ORDER = {"A": "xyz", "B": "yzx", "C": "zxy"}


def pack_kernel(s_ref, q_ref, kv_ref, a_ref, b_ref, c_ref):
    xh, core = s_ref[0], s_ref[1]
    main = pl.ds(pl.multiple_of(64 * core, 64), 256)
    rest = pl.ds(pl.multiple_of(256 * (1 - core), 64), 64)
    q_main, q_rest = q_ref[main, :], q_ref[rest, :]

    def pick(cols, wanted):
        row = lax.broadcasted_iota(jnp.int32, (320, cols), 0)
        col = lax.broadcasted_iota(jnp.int32, (320, cols), 1)
        return jnp.where(wanted(row, col), 1.0, 0.0).astype(BF16)

    def dot(left, right):
        return jnp.dot(left, right, preferred_element_type=F32)

    heads = pick(256, lambda r, j: r == j + 64 * xh)
    start = 256 * (1 - xh)
    upper = pick(128, lambda r, j: (r - start == j - 64 * xh) & (r >= start) & (r < start + 64))
    lower = pick(128, lambda r, j: (r - start == j - 64 * (1 - xh)) & (r >= start) & (r < start + 64))
    t_main = dot(q_main, heads).astype(BF16)
    t_rest = dot(q_rest, heads).astype(BF16)
    a_ref[0:256, :] = t_main[:, :128]
    a_ref[256:320, :] = t_rest[:, :128]
    b_ref[0:256, :] = t_main[:, 128:]
    b_ref[256:320, :] = t_rest[:, 128:]
    a_ref[320:448, :] = (dot(q_main[:128], upper) + dot(q_main[128:], lower)).astype(BF16)
    a_ref[448:480, :] = (dot(q_rest[:32], upper) + dot(q_rest[32:], lower)).astype(BF16)
    c_ref[0:256, :] = kv_ref[main, :]
    c_ref[256:320, :] = kv_ref[rest, :]


def pack(q_weight, kv_weight, scalars):
    return pl.pallas_call(
        pack_kernel,
        grid_spec=pltpu.PrefetchScalarGridSpec(
            num_scalar_prefetch=1,
            grid=(1,),
            in_specs=[
                pl.BlockSpec((320, 320), lambda i, s: (0, 0)),
                pl.BlockSpec((320, 128), lambda i, s: (0, 0)),
            ],
            out_specs=[
                pl.BlockSpec((480, 128), lambda i, s: (0, 0)),
                pl.BlockSpec((320, 128), lambda i, s: (0, 0)),
                pl.BlockSpec((320, 128), lambda i, s: (0, 0)),
            ],
        ),
        out_shape=[
            jax.ShapeDtypeStruct((480, 128), BF16),
            jax.ShapeDtypeStruct((320, 128), BF16),
            jax.ShapeDtypeStruct((320, 128), BF16),
        ],
        name="pack",
    )(scalars, q_weight, kv_weight)


XCOLS = 3072


def norm_kernel(s_ref, h_ref, g_ref, own_ref, sib_ref, n_ref):
    core = s_ref[1]
    h = h_ref[...].astype(F32)
    mean_square = jnp.mean(h * h, axis=-1, keepdims=True)
    n_ref[...] = (h * lax.rsqrt(mean_square + 1e-06) * g_ref[...].astype(F32)).astype(BF16)
    low_lane = lax.broadcasted_iota(jnp.int32, (h.shape[0], 128), 1) < 64
    middle = {}
    for y in range(4):
        for xl in range(2):
            tile = n_ref[:, 640 * (2 * y + xl) + 256 : 640 * (2 * y + xl) + 384].astype(F32)
            middle[y, xl] = (tile, pltpu.roll(tile, 64, 1))
    for out_ref, which in ((own_ref, core), (sib_ref, 1 - core)):
        for xl in range(2):
            for y in range(4):
                start = pl.multiple_of(640 * (2 * y + xl) + 384 * which, 128)
                out_ref[:, (xl * 4 + y) * 256 : (xl * 4 + y + 1) * 256] = n_ref[:, pl.ds(start, 256)]

        def join(first, second):
            left = jnp.where(which == 0, first[0], first[1])
            right = jnp.where(which == 0, second[1], second[0])
            return jnp.where(low_lane, left, right).astype(BF16)

        for xl in range(2):
            for k in range(2):
                at = 2048 + xl * 256 + k * 128
                out_ref[:, at : at + 128] = join(middle[2 * k, xl], middle[2 * k + 1, xl])
        for y in range(4):
            at = 2560 + y * 128
            out_ref[:, at : at + 128] = join(middle[y, 0], middle[y, 1])


def normalize(hidden, norm_gain, scalars):
    out = jax.ShapeDtypeStruct((ROWS, XCOLS), BF16)
    return pl.pallas_call(
        norm_kernel,
        grid_spec=pltpu.PrefetchScalarGridSpec(
            num_scalar_prefetch=1,
            grid=(3,),
            in_specs=[
                pl.BlockSpec((128, D), lambda i, s: (i, 0)),
                pl.BlockSpec((1, D), lambda i, s: (0, 0)),
            ],
            out_specs=[
                pl.BlockSpec((128, XCOLS), lambda i, s: (i, 0)),
                pl.BlockSpec((128, XCOLS), lambda i, s: (i, 0)),
            ],
            scratch_shapes=[pltpu.VMEM((128, D), BF16)],
        ),
        out_shape=[out, out],
        name="norm",
    )(scalars, hidden, norm_gain.reshape(1, D))


def plane_kernel(step, t_ref, *refs):
    (a0, a1, b0, b1, c0, c1, x_own, x_oth), refs = refs[:8], refs[8:]
    prev_b = []
    prev_c = None
    if step == 1 or step == 2:
        prev_b, prev_c, refs = [refs[0]], refs[1], refs[2:]
    elif step == 3:
        prev_b, prev_c, refs = [refs[0], refs[1]], refs[2], refs[3:]
    last = step == 3
    if last:
        a_own, b_own, c_own, sent = refs[:4]
        refs = refs[4:]
    else:
        a_own, a_send, b_out, c_out = refs[:4]
        refs = refs[4:]
    xv, wa, sraw, ws, wb, wc, bp, cp, sems = refs
    pltpu.make_async_copy(x_own, xv.at[0:ROWS], sems.at[0]).start()
    pltpu.make_async_copy(x_oth, xv.at[ROWS : 2 * ROWS], sems.at[1]).start()
    for e, (a_ref, b_ref, c_ref) in enumerate(((a0, b0, c0), (a1, b1, c1))):
        for p in range(8):
            i = e * 8 + p
            slot, col = t_ref[i], t_ref[16 + i]
            lanes = pl.ds(pl.multiple_of(col * 128, 128), 128)
            pltpu.make_async_copy(
                c_ref.at[p, 0:256], wc.at[pl.ds(pl.multiple_of(t_ref[64 + i] * 256, 256), 256), pl.ds(pl.multiple_of(t_ref[80 + i] * 128, 128), 128)], sems.at[2]
            ).start()
            pltpu.make_async_copy(
                c_ref.at[p, 256:320], wc.at[pl.ds(pl.multiple_of(512 + t_ref[64 + i] * 64, 64), 64), pl.ds(pl.multiple_of(t_ref[80 + i] * 128, 128), 128)], sems.at[2]
            ).start()
            pltpu.make_async_copy(
                b_ref.at[p, 0:256], wb.at[pl.ds(pl.multiple_of(t_ref[32 + i] * 256, 256), 256), pl.ds(pl.multiple_of(t_ref[48 + i] * 128, 128), 128)], sems.at[3]
            ).start()
            pltpu.make_async_copy(
                b_ref.at[p, 256:320], wb.at[pl.ds(pl.multiple_of(1024 + t_ref[32 + i] * 64, 64), 64), pl.ds(pl.multiple_of(t_ref[48 + i] * 128, 128), 128)], sems.at[3]
            ).start()
            pltpu.make_async_copy(a_ref.at[p, 0:256], wa.at[pl.ds(pl.multiple_of(slot * 256, 256), 256), lanes], sems.at[4]).start()
            pltpu.make_async_copy(a_ref.at[p, 256:320], wa.at[pl.ds(pl.multiple_of(2048 + slot * 64, 64), 64), lanes], sems.at[4]).start()
            pltpu.make_async_copy(a_ref.at[p, 320:480], sraw.at[col, slot], sems.at[5]).start()
    if prev_c is not None:
        pltpu.make_async_copy(prev_c, cp, sems.at[6]).start()
    core = t_ref[112]
    if step == 1 or step == 2:
        pltpu.make_async_copy(prev_b[0], bp, sems.at[7]).start()
    elif step == 3:

        @pl.when(core == 0)
        def _():
            pltpu.make_async_copy(prev_b[0], bp, sems.at[7]).start()

        @pl.when(core == 1)
        def _():
            pltpu.make_async_copy(prev_b[1], bp, sems.at[7]).start()

    def wait(ref, k):
        pltpu.make_async_copy(ref, ref, sems.at[k]).wait()

    def dot(left, right):
        return jnp.dot(left, right, preferred_element_type=F32)

    def lanes_of(start, size):
        return pl.ds(pl.multiple_of(start, 128), size)

    wait(xv.at[0:ROWS], 0)
    wait(xv.at[ROWS : 2 * ROWS], 1)
    wait(wc, 2)
    y = t_ref[100 + step]
    kv = dot(xv[:, lanes_of(y * 256, 256)], wc[0:256, :])
    kv += dot(xv[:, lanes_of(1024 + y * 256, 256)], wc[256:512, :])
    kv += dot(xv[:, lanes_of(2560 + y * 128, 128)], wc[512:640, :])
    if prev_c is not None:
        wait(cp, 6)
        kv += cp[...]
    if last:
        c_own[...] = kv[:ROWS]
        sent[:, 896:1920] = kv[ROWS:].astype(BF16)
    else:
        c_out[...] = kv
    wait(wb, 3)
    xl = t_ref[96 + step]
    qb = dot(xv[:, lanes_of(xl * 1024, 1024)], wb[0:1024, :])
    qb += dot(xv[:, lanes_of(2048 + xl * 256, 256)], wb[1024:1280, :])
    if step == 1 or step == 2:
        wait(bp, 7)
        keep = jnp.where(core == (0 if step == 1 else 1), 1.0, 0.0)
        qb += bp[...] * keep
    elif step == 3:
        wait(bp, 7)
        qb += bp[...]
    if last:
        b_own[...] = qb[:ROWS]
        sent[:, 384:896] = qb[ROWS:].astype(BF16)
    else:
        b_out[...] = qb
    wait(wa, 4)
    wait(sraw, 5)
    for slot in range(8):
        for rows, at in ((slice(0, 128), slot * 256), (slice(128, 160), 2048 + slot * 64)):
            n = rows.stop - rows.start
            even = sraw[0, slot, rows, :].astype(F32)
            odd = sraw[1, slot, rows, :].astype(F32)
            low_lane = lax.broadcasted_iota(jnp.int32, (n, 128), 1) < 64
            ws[at : at + n, :] = jnp.where(low_lane, even, odd).astype(BF16)
            ws[at + n : at + 2 * n, :] = pltpu.roll(jnp.where(low_lane, odd, even), 64, 1).astype(BF16)
    qa = dot(xv[:, 0:2560], wa[...])
    qs = dot(xv[:, 0:2560], ws[...])
    a_own[:, 0:256] = qa[:ROWS]
    a_own[:, 256:384] = qs[:ROWS]
    if last:
        sent[:, 0:256] = qa[ROWS:].astype(BF16)
        sent[:, 256:384] = qs[ROWS:].astype(BF16)
    else:
        a_send[:, 0:256] = qa[ROWS:].astype(BF16)
        a_send[:, 256:384] = qs[ROWS:].astype(BF16)


def plane(step, table, pieces, x_own, x_oth, prev_b, prev_c):
    hbm = pl.BlockSpec(memory_space=pl.ANY)
    vmem = pl.BlockSpec(memory_space=pltpu.VMEM)
    operands = list(pieces) + [x_own, x_oth] + list(prev_b) + ([] if prev_c is None else [prev_c])
    shape = jax.ShapeDtypeStruct
    if step == 3:
        outs = [shape((ROWS, 384), F32), shape((ROWS, 512), F32), shape((ROWS, 1024), F32), shape((ROWS, 1920), BF16)]
    else:
        outs = [shape((ROWS, 384), F32), shape((ROWS, 384), BF16), shape((2 * ROWS, 512), F32), shape((2 * ROWS, 1024), F32)]

    def body(*refs):
        plane_kernel(step, *refs)

    return pl.pallas_call(
        body,
        grid_spec=pltpu.PrefetchScalarGridSpec(
            num_scalar_prefetch=1,
            grid=(),
            in_specs=[hbm] * len(operands),
            out_specs=[vmem] * 4,
            scratch_shapes=[
                pltpu.VMEM((2 * ROWS, XCOLS), BF16),
                pltpu.VMEM((2560, 256), BF16),
                pltpu.VMEM((2, 8, 160, 128), BF16),
                pltpu.VMEM((2560, 128), BF16),
                pltpu.VMEM((1280, 512), BF16),
                pltpu.VMEM((640, 1024), BF16),
                pltpu.VMEM((2 * ROWS, 512), F32),
                pltpu.VMEM((2 * ROWS, 1024), F32),
                pltpu.SemaphoreType.DMA((8,)),
            ],
        ),
        out_shape=outs,
        name=f"plane{step}",
    )(table, *operands)


def attend_kernel(t_ref, own012, own3, own_b1, own_b2, own_k, own_v, got012, got3, got_b1, got_b2, got_k, got_v, cos_ref, sin_ref, qb_ref, kvb_ref, segc_ref, segr_ref, out_ref, qs_ref):
    i = pl.program_id(0)
    z = t_ref[104 + i]
    xh = t_ref[113]
    cos, sin = cos_ref[...], sin_ref[...]

    def bias_of(ref, tile):
        return ref[:, pl.ds(pl.multiple_of(tile * 128, 128), 128)].astype(F32)

    def rotary(x):
        return x * cos + pltpu.roll(x, 64, 1) * sin

    final = i == 3
    heads = []
    for k, h in ((0, 0), (1, 3), (2, 2)):
        own = jnp.where(final, own3[:, k * 128 : k * 128 + 128], own012[:, k * 128 : k * 128 + 128])
        got = jnp.where(final, got3[:, k * 128 : k * 128 + 128].astype(F32), got012[:, k * 128 : k * 128 + 128].astype(F32))
        heads.append((own + got, jnp.int32(h)))
    heads.append((own_b1[...] + got_b1[...].astype(F32), 1 + 3 * xh))
    heads.append((own_b2[...] + got_b2[...].astype(F32), 4 - 3 * xh))
    for n, (lin, h) in enumerate(heads):
        qs_ref[n] = rotary(lin + bias_of(qb_ref, 5 * z + h)).astype(BF16)
    key = rotary(own_k[...] + got_k[...].astype(F32) + bias_of(kvb_ref, z)).astype(BF16)
    value = (own_v[...] + got_v[...].astype(F32) + bias_of(kvb_ref, 4 + z)).astype(BF16)
    for b in range(3):
        rows = slice(b * 128, b * 128 + 128)
        width = b * 128 + 128
        row = lax.broadcasted_iota(jnp.int32, (128, width), 0) + b * 128
        col = lax.broadcasted_iota(jnp.int32, (128, width), 1)
        seg = segc_ref[rows, :]
        allowed = (seg == segr_ref[:, :width]) & (col <= row) & (seg >= 0)
        live = seg >= 0
        for n, (_, h) in enumerate(heads):
            scores = lax.dot_general(qs_ref[n, rows, :], key[:width], (((1,), (1,)), ((), ())), preferred_element_type=F32) * HEAD_DIM ** (-0.5)
            scores = jnp.where(allowed, scores, -1e30)
            exponents = jnp.exp(scores - jnp.max(scores, axis=-1, keepdims=True))
            probabilities = (exponents / jnp.sum(exponents, axis=-1, keepdims=True)).astype(BF16)
            context = jnp.dot(probabilities, value[:width], preferred_element_type=F32)
            out_ref[rows, pl.ds(pl.multiple_of(h * 128, 128), 128)] = jnp.where(live, context, 0.0).astype(BF16)


def attend(table, own012, own3, own_b1, own_b2, own_kv, got_early, got_late, cos, sin, q_bias, kv_bias, segments):
    whole = lambda i, t: (0, 0)
    other = lambda i, t: (0, jnp.where(i == 1, 2, jnp.where(i == 2, 1, 0)))
    narrow = lambda first: pl.BlockSpec((ROWS, 128), lambda i, t: (0, first + t[104 + i]))
    return pl.pallas_call(
        attend_kernel,
        grid_spec=pltpu.PrefetchScalarGridSpec(
            num_scalar_prefetch=1,
            grid=(4,),
            in_specs=[
                pl.BlockSpec((ROWS, 384), lambda i, t: (0, jnp.minimum(i, 2))),
                pl.BlockSpec((ROWS, 384), whole),
                narrow(0),
                narrow(0),
                narrow(0),
                narrow(4),
                pl.BlockSpec((ROWS, 384), other),
                pl.BlockSpec((ROWS, 384), whole),
                narrow(9),
                narrow(3),
                narrow(7),
                narrow(11),
                pl.BlockSpec((ROWS, 128), whole),
                pl.BlockSpec((ROWS, 128), whole),
                pl.BlockSpec((1, 2560), whole),
                pl.BlockSpec((1, 1024), whole),
                pl.BlockSpec((ROWS, 1), whole),
                pl.BlockSpec((1, ROWS), whole),
            ],
            out_specs=pl.BlockSpec((ROWS, 640), lambda i, t: (0, t[104 + i])),
            scratch_shapes=[pltpu.VMEM((5, ROWS, 128), BF16)],
        ),
        out_shape=jax.ShapeDtypeStruct((ROWS, 2560), BF16),
        name="attend",
    )(
        table, own012, own3, own_b1, own_b2, own_kv, own_kv, got_early, got_late, got_early, got_late, got_late, got_late,
        cos, sin, q_bias.reshape(1, -1), kv_bias.reshape(1, -1), segments.reshape(-1, 1), segments.reshape(1, -1),
    )


def positions_of(segments):
    row_ids = jnp.arange(segments.shape[0], dtype=jnp.int32)
    same = segments[:, None] == segments[None, :]
    return row_ids - jnp.min(jnp.where(same, row_ids[None, :], segments.shape[0]), axis=1)


def rotary_tables(segments):
    half_dim = HEAD_DIM // 2
    frequency = jnp.exp(jnp.arange(half_dim, dtype=F32) * (-2.0 / HEAD_DIM) * jnp.log(jnp.float32(1000000.0)))
    angles = positions_of(segments).astype(F32)[:, None] * frequency[None, :]
    cos, sin = jnp.cos(angles), jnp.sin(angles)
    return jnp.concatenate([cos, cos], axis=1), jnp.concatenate([-sin, sin], axis=1)


def place_table(y, x, z, core):
    rows = [[] for _ in range(6)]
    for i in range(16):
        b1, b2, b3, b4 = i & 1, (i >> 1) & 1, (i >> 2) & 1, i >> 3
        ax = ring_source(x, core, b1, b2)
        ay = ring_source(y, core, b3, b4)
        rows[0].append((ax % 2) * 4 + ay)
        rows[1].append(ax // 2)
        by = ring_source(y, core, b1, b2)
        bz = ring_source(z, core, b3, b4)
        rows[2].append(by)
        rows[3].append(bz)
        cz = ring_source(z, core, b1, b2)
        cx = ring_source(x, core, b3, b4)
        rows[4].append(cx % 2)
        rows[5].append(cz * 2 + cx // 2)
    planes = [(s & 1, s >> 1) for s in range(4)]
    flat = [v for row in rows for v in row]
    flat += [ring_source(x, core, *b) % 2 for b in planes]
    flat += [ring_source(y, core, *b) for b in planes]
    flat += [ring_source(z, core, *b) for b in planes]
    flat += [jnp.int32(0)] * 4
    flat += [core, x // 2] + [jnp.int32(0)] * 2
    return jnp.stack([jnp.asarray(v, jnp.int32) for v in flat])


def local(hidden, norm_gain, q_weight, kv_weight, q_bias, kv_bias, segments):
    y, xl, core = lax.axis_index("y"), lax.axis_index("xl"), lax.axis_index("c")
    z, xh = lax.axis_index("z"), lax.axis_index("xh")
    x = 2 * xh + xl
    scalars = jnp.stack([xh, core]).astype(jnp.int32)
    table = place_table(y, x, z, core)

    def send(value, part, dim):
        return lax.ppermute(value, AXES, exchange_pairs(AXIS_ORDER[part][dim // 2], dim % 2))

    held = dict(zip("ABC", pack(q_weight, kv_weight, scalars)))
    held = {k: v[None] for k, v in held.items()}
    x_own, x_sib = normalize(hidden, norm_gain, scalars)
    x_oth = lax.ppermute(x_sib, "c", [(0, 1), (1, 0)])
    for dim in range(3):
        got = {k: send(v, k, dim) for k, v in held.items()}
        held = {k: jnp.concatenate([held[k], got[k]], axis=0) for k in "ABC"}
    parts = {k: [held[k]] for k in "ABC"}
    for dim in range(3, 6):
        for i in range(2 ** (dim - 3)):
            for k in "ABC":
                parts[k].append(send(parts[k][i], k, dim))

    cos, sin = rotary_tables(segments)
    own_a, send_a, out_b = [], [], []
    acc = None
    for step in range(4):
        pieces = [parts[k][2 * step + e] for k in "ABC" for e in range(2)]
        prev = [] if step == 0 else [out_b[0]] if step < 3 else [out_b[2], out_b[1]]
        res = plane(step, table, pieces, x_own, x_oth, prev, acc)
        own_a.append(res[0])
        if step < 3:
            send_a.append(res[1])
            out_b.append(res[2])
            acc = res[3]
    first_b = jnp.where(core == 0, out_b[1], out_b[2])
    early = jnp.concatenate(send_a + [first_b[ROWS:].astype(BF16)], axis=1)
    own012 = jnp.concatenate(own_a[:3], axis=1)
    swap = [(0, 1), (1, 0)]
    got_early = lax.ppermute(early, "c", swap)
    got_late = lax.ppermute(res[3], "c", swap)
    return attend(table, own012, own_a[3], first_b[:ROWS], res[1], res[2], got_early, got_late, cos, sin, q_bias, kv_bias, segments)


def solution(mesh):
    torus = Mesh(mesh.devices.reshape(4, 2, 2, 4, 2), AXES)
    rows = P(AXES)
    weights = P(("y", "xl", "c"), ("z", "xh"))
    return jax.shard_map(
        local,
        mesh=torus,
        in_specs=(P(AXES, None), P(), weights, weights, P(), P(), rows),
        out_specs=P(AXES, None),
        check_vma=False,
    )
```

```python
import jax
import jax.numpy as jnp
from jax import lax
from jax.experimental import pallas as pl
from jax.experimental.pallas import tpu as pltpu
from jax.sharding import Mesh, PartitionSpec as P


HEAD_DIM = 128
ROWS = 384
D = 5120
AXES = ("y", "xl", "c", "z", "xh")
F32 = jnp.float32
BF16 = jnp.bfloat16


def pair_low(v):
    return v ^ 1


def pair_high(v):
    return (v + 1) % 4 if v % 2 else (v - 1) % 4


def pair_of(order, core):
    return pair_low if (order + core) % 2 == 0 else pair_high


def exchange_pairs(axis, order):
    pairs = []
    for y in range(4):
        for xl in range(2):
            for c in range(2):
                for z in range(4):
                    for xh in range(2):
                        move = pair_of(order, c)
                        ty, tx, tz = y, 2 * xh + xl, z
                        if axis == "x":
                            tx = move(tx)
                        elif axis == "y":
                            ty = move(ty)
                        else:
                            tz = move(tz)
                        src = (((y * 2 + xl) * 2 + c) * 4 + z) * 2 + xh
                        dst = (((ty * 2 + tx % 2) * 2 + c) * 4 + tz) * 2 + tx // 2
                        pairs.append((src, dst))
    return pairs


def traced_pair(v, order, core):
    low = v ^ 1
    high = jnp.where(v % 2 == 1, v + 1, v + 3) % 4
    return jnp.where((core + order) % 2 == 0, low, high)


def ring_source(v, core, first, second):
    if second:
        v = traced_pair(v, 1, core)
    if first:
        v = traced_pair(v, 0, core)
    return v


AXIS_ORDER = {"A": "xyz", "B": "yzx", "C": "zxy"}


def pack_kernel(s_ref, q_ref, kv_ref, a_ref, b_ref, c_ref):
    xh, core = s_ref[0], s_ref[1]
    main = pl.ds(pl.multiple_of(64 * core, 64), 256)
    rest = pl.ds(pl.multiple_of(256 * (1 - core), 64), 64)
    q_main, q_rest = q_ref[main, :], q_ref[rest, :]

    def pick(cols, wanted):
        row = lax.broadcasted_iota(jnp.int32, (320, cols), 0)
        col = lax.broadcasted_iota(jnp.int32, (320, cols), 1)
        return jnp.where(wanted(row, col), 1.0, 0.0).astype(BF16)

    def dot(left, right):
        return jnp.dot(left, right, preferred_element_type=F32)

    heads = pick(256, lambda r, j: r == j + 64 * xh)
    start = 256 * (1 - xh)
    upper = pick(128, lambda r, j: (r - start == j - 64 * xh) & (r >= start) & (r < start + 64))
    lower = pick(128, lambda r, j: (r - start == j - 64 * (1 - xh)) & (r >= start) & (r < start + 64))
    t_main = dot(q_main, heads).astype(BF16)
    t_rest = dot(q_rest, heads).astype(BF16)
    a_ref[0:256, :] = t_main[:, :128]
    a_ref[256:320, :] = t_rest[:, :128]
    b_ref[0:256, :] = t_main[:, 128:]
    b_ref[256:320, :] = t_rest[:, 128:]
    a_ref[320:448, :] = (dot(q_main[:128], upper) + dot(q_main[128:], lower)).astype(BF16)
    a_ref[448:480, :] = (dot(q_rest[:32], upper) + dot(q_rest[32:], lower)).astype(BF16)
    c_ref[0:256, :] = kv_ref[main, :]
    c_ref[256:320, :] = kv_ref[rest, :]


def pack(q_weight, kv_weight, scalars):
    return pl.pallas_call(
        pack_kernel,
        grid_spec=pltpu.PrefetchScalarGridSpec(
            num_scalar_prefetch=1,
            grid=(1,),
            in_specs=[
                pl.BlockSpec((320, 320), lambda i, s: (0, 0)),
                pl.BlockSpec((320, 128), lambda i, s: (0, 0)),
            ],
            out_specs=[
                pl.BlockSpec((480, 128), lambda i, s: (0, 0)),
                pl.BlockSpec((320, 128), lambda i, s: (0, 0)),
                pl.BlockSpec((320, 128), lambda i, s: (0, 0)),
            ],
        ),
        out_shape=[
            jax.ShapeDtypeStruct((480, 128), BF16),
            jax.ShapeDtypeStruct((320, 128), BF16),
            jax.ShapeDtypeStruct((320, 128), BF16),
        ],
        name="pack",
    )(scalars, q_weight, kv_weight)


XCOLS = 3072


def norm_kernel(s_ref, h_ref, g_ref, _, own_ref, sib_ref, n_ref):
    core = s_ref[1]
    h = h_ref[...].astype(F32)
    mean_square = jnp.mean(h * h, axis=-1, keepdims=True)
    n_ref[...] = (h * lax.rsqrt(mean_square + 1e-06) * g_ref[...].astype(F32)).astype(BF16)
    low_lane = lax.broadcasted_iota(jnp.int32, (h.shape[0], 128), 1) < 64
    middle = {}
    for y in range(4):
        for xl in range(2):
            tile = n_ref[:, 640 * (2 * y + xl) + 256 : 640 * (2 * y + xl) + 384].astype(F32)
            middle[y, xl] = (tile, pltpu.roll(tile, 64, 1))
    for out_ref, which in ((own_ref, core), (sib_ref, 1 - core)):
        for xl in range(2):
            for y in range(4):
                start = pl.multiple_of(640 * (2 * y + xl) + 384 * which, 128)
                out_ref[:, (xl * 4 + y) * 256 : (xl * 4 + y + 1) * 256] = n_ref[:, pl.ds(start, 256)]

        def join(first, second):
            left = jnp.where(which == 0, first[0], first[1])
            right = jnp.where(which == 0, second[1], second[0])
            return jnp.where(low_lane, left, right).astype(BF16)

        for xl in range(2):
            for k in range(2):
                at = 2048 + xl * 256 + k * 128
                out_ref[:, at : at + 128] = join(middle[2 * k, xl], middle[2 * k + 1, xl])
        for y in range(4):
            at = 2560 + y * 128
            out_ref[:, at : at + 128] = join(middle[y, 0], middle[y, 1])


def normalize(hidden, norm_gain, scalars, after):
    out = jax.ShapeDtypeStruct((ROWS, XCOLS), BF16)
    return pl.pallas_call(
        norm_kernel,
        grid_spec=pltpu.PrefetchScalarGridSpec(
            num_scalar_prefetch=1,
            grid=(3,),
            in_specs=[
                pl.BlockSpec((128, D), lambda i, s: (i, 0)),
                pl.BlockSpec((1, D), lambda i, s: (0, 0)),
                pl.BlockSpec(memory_space=pl.ANY),
            ],
            out_specs=[
                pl.BlockSpec((128, XCOLS), lambda i, s: (i, 0)),
                pl.BlockSpec((128, XCOLS), lambda i, s: (i, 0)),
            ],
            scratch_shapes=[pltpu.VMEM((128, D), BF16)],
        ),
        out_shape=[out, out],
        name="norm",
        cost_estimate=pl.CostEstimate(flops=10_000_000, transcendentals=0, bytes_accessed=9_000_000),
    )(scalars, hidden, norm_gain.reshape(1, D), after)


def stack_kernel(*refs):
    held, got, outs = refs[:3], refs[3:6], refs[-3:]
    for k in range(3):
        n = held[k].shape[0]
        outs[k][0:n] = held[k][...]
        outs[k][n : 2 * n] = got[k][...]


def stack(held, got, after=()):
    hbm = pl.BlockSpec(memory_space=pl.ANY)
    vmem = pl.BlockSpec(memory_space=pltpu.VMEM)
    names = "ABC"
    shapes = [jax.ShapeDtypeStruct((2 * held[k].shape[0],) + held[k].shape[1:], BF16) for k in names]
    operands = [held[k] for k in names] + [got[k] for k in names] + list(after)
    outs = pl.pallas_call(
        stack_kernel,
        in_specs=[vmem] * 6 + [hbm] * len(after),
        out_specs=[vmem] * 3,
        out_shape=shapes,
        name="stack",
        cost_estimate=pl.CostEstimate(flops=0, transcendentals=0, bytes_accessed=sum(4 * v.size for v in held.values()) * 2),
    )(*operands)
    return dict(zip(names, outs))


EARLY = 13
LATE = 15


def plane_kernel(step, n_in, t_ref, *refs):
    last = step == 3
    ins, outs = refs[:n_in], list(refs[n_in : n_in + (4 if last else 5)])
    xv, wa, sraw, ws, wb, wc, bp, cp, own_s, sib_s, sems, out_sems = refs[n_in + len(outs) :]
    a0, a1, b0, b1, c0, c1, x_own, x_oth = ins[:8]
    prev_b, prev_c = [], None
    if step in (1, 2):
        prev_b, prev_c = [ins[8]], ins[9]
    elif last:
        prev_b, prev_c = [ins[8], ins[9]], ins[10]
    pltpu.make_async_copy(x_own, xv.at[0:ROWS], sems.at[0]).start()
    pltpu.make_async_copy(x_oth, xv.at[ROWS : 2 * ROWS], sems.at[1]).start()

    def rows_at(start, size):
        return pl.ds(pl.multiple_of(start, size), size)

    def lanes_of(start, size):
        return pl.ds(pl.multiple_of(start, 128), size)

    places = [(e, p) for e in range(2) for p in range(8)]
    for e, p in places:
        row, col = t_ref[64 + e * 8 + p], lanes_of(t_ref[80 + e * 8 + p] * 128, 128)
        src = (c0, c1)[e]
        pltpu.make_async_copy(src.at[p, 0:256], wc.at[rows_at(row * 256, 256), col], sems.at[2]).start()
        pltpu.make_async_copy(src.at[p, 256:320], wc.at[rows_at(512 + row * 64, 64), col], sems.at[2]).start()
    if prev_c is not None:
        pltpu.make_async_copy(prev_c, cp, sems.at[6]).start()
    for e, p in places:
        row, col = t_ref[32 + e * 8 + p], lanes_of(t_ref[48 + e * 8 + p] * 128, 128)
        src = (b0, b1)[e]
        pltpu.make_async_copy(src.at[p, 0:256], wb.at[rows_at(row * 256, 256), col], sems.at[3]).start()
        pltpu.make_async_copy(src.at[p, 256:320], wb.at[rows_at(1024 + row * 64, 64), col], sems.at[3]).start()
    core = t_ref[112]
    if step in (1, 2):
        pltpu.make_async_copy(prev_b[0], bp, sems.at[7]).start()
    elif last:
        for k in range(2):

            @pl.when(core == k)
            def _():
                pltpu.make_async_copy(prev_b[k], bp, sems.at[7]).start()

    for e, p in places:
        row, which = t_ref[e * 8 + p], t_ref[16 + e * 8 + p]
        col = lanes_of(which * 128, 128)
        src = (a0, a1)[e]
        pltpu.make_async_copy(src.at[p, 0:256], wa.at[rows_at(row * 256, 256), col], sems.at[4]).start()
        pltpu.make_async_copy(src.at[p, 256:320], wa.at[rows_at(2048 + row * 64, 64), col], sems.at[4]).start()
        pltpu.make_async_copy(src.at[p, 320:480], sraw.at[which, row], sems.at[5]).start()

    def wait(ref, k):
        pltpu.make_async_copy(ref, ref, sems.at[k]).wait()

    def dot(left, right):
        return jnp.dot(left, right, preferred_element_type=F32)

    def split(value, at, tiles):
        for k in range(tiles):
            own_s[at + k] = value[:ROWS, k * 128 : k * 128 + 128]
            sib_s[at + k] = value[ROWS:, k * 128 : k * 128 + 128].astype(BF16)

    def copies_out(pairs):
        return [pltpu.make_async_copy(src, dst, out_sems.at[k]) for src, dst, k in pairs]

    wait(xv.at[0:ROWS], 0)
    wait(xv.at[ROWS : 2 * ROWS], 1)
    if last:
        own_a, own_b, own_kv, late = outs
    else:
        own_a, own_b, early, b_out, c_out = outs
    done = []
    wait(wc, 2)
    y = t_ref[100 + step]
    kv = dot(xv[:, lanes_of(y * 256, 256)], wc[0:256, :])
    kv += dot(xv[:, lanes_of(1024 + y * 256, 256)], wc[256:512, :])
    kv += dot(xv[:, lanes_of(2560 + y * 128, 128)], wc[512:640, :])
    if prev_c is not None:
        wait(cp, 6)
        kv += cp[...]
    if last:
        split(kv, 7, 8)
        out = copies_out([(own_s.at[7:15], own_kv, 0), (sib_s.at[7:15], late.at[7:15], 1)])
    else:
        cp[...] = kv
        out = copies_out([(cp, c_out, 0)])
    for copy in out:
        copy.start()
    done += out
    wait(wb, 3)
    xl = t_ref[96 + step]
    qb = dot(xv[:, lanes_of(xl * 1024, 1024)], wb[0:1024, :])
    qb += dot(xv[:, lanes_of(2048 + xl * 256, 256)], wb[1024:1280, :])
    if step in (1, 2):
        wait(bp, 7)
        qb += jnp.where(core == step - 1, bp[...], 0.0)
    elif last:
        wait(bp, 7)
        qb += bp[...]
    if last:
        split(qb, 3, 4)
        out = copies_out([(own_s.at[3:7], own_b.at[4:8], 2), (sib_s.at[3:7], late.at[3:7], 3)])
        for copy in out:
            copy.start()
        done += out
    else:
        bp[...] = qb
        out = copies_out([(bp, b_out, 2)])
        out[0].start()
        done += out
        if step in (1, 2):
            split(qb, 3, 4)

            @pl.when(core == step - 1)
            def _():
                for copy in copies_out([(own_s.at[3:7], own_b.at[0:4], 3), (sib_s.at[3:7], early.at[9:13], 4)]):
                    copy.start()

    wait(wa, 4)
    wait(sraw, 5)
    for slot in range(8):
        for rows, at in ((slice(0, 128), slot * 256), (slice(128, 160), 2048 + slot * 64)):
            n = rows.stop - rows.start
            even = sraw[0, slot, rows, :].astype(F32)
            odd = sraw[1, slot, rows, :].astype(F32)
            low_lane = lax.broadcasted_iota(jnp.int32, (n, 128), 1) < 64
            ws[at : at + n, :] = jnp.where(low_lane, even, odd).astype(BF16)
            ws[at + n : at + 2 * n, :] = pltpu.roll(jnp.where(low_lane, odd, even), 64, 1).astype(BF16)
    split(dot(xv[:, 0:2560], wa[...]), 0, 2)
    split(dot(xv[:, 0:2560], ws[...]), 2, 1)
    sent = late.at[0:3] if last else early.at[3 * step : 3 * step + 3]
    out = copies_out([(own_s.at[0:3], own_a.at[3 * step : 3 * step + 3], 5), (sib_s.at[0:3], sent, 6)])
    for copy in out:
        copy.start()
    done += out
    for copy in done:
        copy.wait()
    if step in (1, 2):

        @pl.when(core == step - 1)
        def _():
            for copy in copies_out([(own_s.at[3:7], own_b.at[0:4], 3), (sib_s.at[3:7], early.at[9:13], 4)]):
                copy.wait()


def plane(step, table, pieces, x_own, x_oth, prev_b, prev_c, chain, after=()):
    hbm = pl.BlockSpec(memory_space=pl.ANY)
    last = step == 3
    shape = jax.ShapeDtypeStruct
    own_a, own_b = shape((12, ROWS, 128), F32), shape((8, ROWS, 128), F32)
    if last:
        outs = [own_a, own_b, shape((8, ROWS, 128), F32), shape((LATE, ROWS, 128), BF16)]
    else:
        outs = [own_a, own_b, shape((EARLY, ROWS, 128), BF16), shape((2 * ROWS, 512), F32), shape((2 * ROWS, 1024), F32)]
    operands = list(pieces) + [x_own, x_oth] + list(prev_b) + ([] if prev_c is None else [prev_c])
    aliases = {}
    if chain is not None:
        for k, v in enumerate(chain[:2] if last else chain):
            aliases[1 + len(operands)] = k
            operands.append(v)
    operands += list(after)
    n_in = len(operands)

    def body(*refs):
        plane_kernel(step, n_in, *refs)

    return pl.pallas_call(
        body,
        grid_spec=pltpu.PrefetchScalarGridSpec(
            num_scalar_prefetch=1,
            grid=(),
            in_specs=[hbm] * n_in,
            out_specs=[hbm] * len(outs),
            scratch_shapes=[
                pltpu.VMEM((2 * ROWS, XCOLS), BF16),
                pltpu.VMEM((2560, 256), BF16),
                pltpu.VMEM((2, 8, 160, 128), BF16),
                pltpu.VMEM((2560, 128), BF16),
                pltpu.VMEM((1280, 512), BF16),
                pltpu.VMEM((640, 1024), BF16),
                pltpu.VMEM((2 * ROWS, 512), F32),
                pltpu.VMEM((2 * ROWS, 1024), F32),
                pltpu.VMEM((15, ROWS, 128), F32),
                pltpu.VMEM((15, ROWS, 128), BF16),
                pltpu.SemaphoreType.DMA((8,)),
                pltpu.SemaphoreType.DMA((7,)),
            ],
        ),
        out_shape=outs,
        input_output_aliases=aliases,
        cost_estimate=pl.CostEstimate(flops=3_500_000_000, transcendentals=0, bytes_accessed=20_000_000),
    )(table, *operands)


def attend_kernel(t_ref, own_a, own_b1, own_b2, own_k, own_v, got_a, got_a3, got_b1, got_b2, got_k, got_v, cos_ref, sin_ref, qb_ref, kvb_ref, segc_ref, segr_ref, out_ref, qs_ref):
    i = pl.program_id(0)
    z = t_ref[104 + i]
    xh = t_ref[113]
    cos, sin = cos_ref[...], sin_ref[...]

    def bias_of(ref, tile):
        return ref[:, pl.ds(pl.multiple_of(tile * 128, 128), 128)].astype(F32)

    def rotary(x):
        return x * cos + pltpu.roll(x, 64, 1) * sin

    heads = []
    for k, h in ((0, 0), (1, 3), (2, 2)):
        got = jnp.where(i == 3, got_a3[k].astype(F32), got_a[k].astype(F32))
        heads.append((own_a[k] + got, h))
    heads.append((own_b1[...] + got_b1[...].astype(F32), 1 + 3 * xh))
    heads.append((own_b2[...] + got_b2[...].astype(F32), 4 - 3 * xh))
    for n, (lin, h) in enumerate(heads):
        qs_ref[n] = rotary(lin + bias_of(qb_ref, 5 * z + h)).astype(BF16)
    key = rotary(own_k[...] + got_k[...].astype(F32) + bias_of(kvb_ref, z)).astype(BF16)
    value = (own_v[...] + got_v[...].astype(F32) + bias_of(kvb_ref, 4 + z)).astype(BF16)
    for b in range(3):
        rows = slice(b * 128, b * 128 + 128)
        width = b * 128 + 128
        row = lax.broadcasted_iota(jnp.int32, (128, width), 0) + b * 128
        col = lax.broadcasted_iota(jnp.int32, (128, width), 1)
        seg = segc_ref[rows, :]
        allowed = (seg == segr_ref[:, :width]) & (col <= row) & (seg >= 0)
        queries = qs_ref[:, rows, :].reshape(5 * 128, 128)
        scores = lax.dot_general(queries, key[:width], (((1,), (1,)), ((), ())), preferred_element_type=F32)
        scores = jnp.where(allowed[None], scores.reshape(5, 128, width), -1e30)
        peak = jnp.max(scores, axis=-1, keepdims=True)
        exponents = jnp.exp2((scores - peak) * (HEAD_DIM ** (-0.5) * 1.4426950408889634))
        share = 1.0 / jnp.sum(exponents, axis=-1, keepdims=True)
        probabilities = (exponents * share).astype(BF16).reshape(5 * 128, width)
        context = jnp.dot(probabilities, value[:width], preferred_element_type=F32).reshape(5, 128, 128)
        context = jnp.where((seg >= 0)[None], context, 0.0).astype(BF16)
        for n, (_, h) in enumerate(heads):
            at = slice(h * 128, h * 128 + 128) if isinstance(h, int) else pl.ds(pl.multiple_of(h * 128, 128), 128)
            out_ref[rows, at] = context[n]


def attend(table, own_a, own_b, own_kv, got_early, got_late, cos, sin, q_bias, kv_bias, segc, segr):
    whole = lambda i, t: (0, 0)
    other = lambda i, t: (jnp.where(i == 1, 2, jnp.where(i == 2, 1, 0)), 0, 0)
    one = lambda first: pl.BlockSpec((None, ROWS, 128), lambda i, t: (first + t[104 + i], 0, 0))
    three = lambda index: pl.BlockSpec((3, ROWS, 128), index)
    return pl.pallas_call(
        attend_kernel,
        grid_spec=pltpu.PrefetchScalarGridSpec(
            num_scalar_prefetch=1,
            grid=(4,),
            in_specs=[
                three(lambda i, t: (i, 0, 0)),
                one(0),
                one(4),
                one(0),
                one(4),
                three(other),
                three(lambda i, t: (0, 0, 0)),
                one(9),
                one(3),
                one(7),
                one(11),
                pl.BlockSpec((ROWS, 128), whole),
                pl.BlockSpec((ROWS, 128), whole),
                pl.BlockSpec((1, 2560), whole),
                pl.BlockSpec((1, 1024), whole),
                pl.BlockSpec((ROWS, 1), whole),
                pl.BlockSpec((1, ROWS), whole),
            ],
            out_specs=pl.BlockSpec((ROWS, 640), lambda i, t: (0, t[104 + i])),
            scratch_shapes=[pltpu.VMEM((5, ROWS, 128), BF16)],
        ),
        out_shape=jax.ShapeDtypeStruct((ROWS, 2560), BF16),
        name="attend",
        cost_estimate=pl.CostEstimate(flops=1_500_000_000, transcendentals=3_000_000, bytes_accessed=11_000_000),
    )(
        table, own_a, own_b, own_b, own_kv, own_kv, got_early, got_late, got_early, got_late, got_late, got_late,
        cos, sin, q_bias, kv_bias, segc, segr,
    )


def positions_of(segments):
    row_ids = jnp.arange(segments.shape[0], dtype=jnp.int32)
    same = segments[:, None] == segments[None, :]
    return row_ids - jnp.min(jnp.where(same, row_ids[None, :], segments.shape[0]), axis=1)


def rotary_tables(segments):
    half_dim = HEAD_DIM // 2
    frequency = jnp.exp(jnp.arange(half_dim, dtype=F32) * (-2.0 / HEAD_DIM) * jnp.log(jnp.float32(1000000.0)))
    angles = positions_of(segments).astype(F32)[:, None] * frequency[None, :]
    cos, sin = jnp.cos(angles), jnp.sin(angles)
    return jnp.concatenate([cos, cos], axis=1), jnp.concatenate([-sin, sin], axis=1)


def place_table(y, x, z, core):
    rows = [[] for _ in range(6)]
    for i in range(16):
        b1, b2, b3, b4 = i & 1, (i >> 1) & 1, (i >> 2) & 1, i >> 3
        ax = ring_source(x, core, b1, b2)
        ay = ring_source(y, core, b3, b4)
        rows[0].append((ax % 2) * 4 + ay)
        rows[1].append(ax // 2)
        by = ring_source(y, core, b1, b2)
        bz = ring_source(z, core, b3, b4)
        rows[2].append(by)
        rows[3].append(bz)
        cz = ring_source(z, core, b1, b2)
        cx = ring_source(x, core, b3, b4)
        rows[4].append(cx % 2)
        rows[5].append(cz * 2 + cx // 2)
    planes = [(s & 1, s >> 1) for s in range(4)]
    flat = [v for row in rows for v in row]
    flat += [ring_source(x, core, *b) % 2 for b in planes]
    flat += [ring_source(y, core, *b) for b in planes]
    flat += [ring_source(z, core, *b) for b in planes]
    flat += [jnp.int32(0)] * 4
    flat += [core, x // 2] + [jnp.int32(0)] * 2
    return jnp.stack([jnp.asarray(v, jnp.int32) for v in flat])


def scorer(hidden, norm_gain, q_weight, kv_weight, q_bias, kv_bias, segments):
    y, xl, core = lax.axis_index("y"), lax.axis_index("xl"), lax.axis_index("c")
    z, xh = lax.axis_index("z"), lax.axis_index("xh")
    x = 2 * xh + xl
    scalars = jnp.stack([xh, core]).astype(jnp.int32)
    table = place_table(y, x, z, core)

    def send(value, part, dim):
        return lax.ppermute(value, AXES, exchange_pairs(AXIS_ORDER[part][dim // 2], dim % 2))

    swap = [(0, 1), (1, 0)]
    held = dict(zip("ABC", pack(q_weight, kv_weight, scalars)))
    held = {k: v[None] for k, v in held.items()}
    got = {k: send(held[k], k, 0) for k in "ABC"}
    held = stack(held, got)
    got = {k: send(held[k], k, 1) for k in "ABC"}
    held = stack(held, got)
    got = {k: send(held[k], k, 2) for k in "ABC"}
    cos, sin = rotary_tables(segments)
    small = [cos, sin, q_bias.reshape(1, -1), kv_bias.reshape(1, -1), segments.reshape(-1, 1), segments.reshape(1, -1)]
    held = stack(held, got)
    x_own, x_sib = normalize(hidden, norm_gain, scalars, held["C"])
    x_oth = lax.ppermute(x_sib, "c", swap)
    parts = {k: [held[k]] for k in "ABC"}
    for dim in range(3, 6):
        for i in range(2 ** (dim - 3)):
            for k in "ABC":
                parts[k].append(send(parts[k][i], k, dim))

    out_b, acc, chain, got_early = [], None, None, None
    for step in range(4):
        pieces = [parts[k][2 * step + e] for k in "ABC" for e in range(2)]
        prev = [] if step == 0 else [out_b[0]] if step < 3 else [out_b[2], out_b[1]]
        res = plane(step, table, pieces, x_own, x_oth, prev, acc, chain, (got_early,) if step == 3 else small if step == 1 else ())
        if step < 3:
            chain = res[:3]
            out_b.append(res[3])
            acc = res[4]
        if step == 2:
            got_early = lax.ppermute(res[2], "c", swap)
    got_late = lax.ppermute(res[3], "c", swap)
    return attend(table, res[0], res[1], res[2], got_early, got_late, *small)


def solution(mesh):
    torus = Mesh(mesh.devices.reshape(4, 2, 2, 4, 2), AXES)
    rows = P(AXES)
    weights = P(("y", "xl", "c"), ("z", "xh"))
    return jax.shard_map(
        scorer,
        mesh=torus,
        in_specs=(P(AXES, None), P(), weights, weights, P(), P(), rows),
        out_specs=P(AXES, None),
        check_vma=False,
    )
```
